256 devices in a mesh: users: 32 (over x, z), rb: 8 (over y, core).
Axes of the slice: x: 4, y: 4, z: 8, core: 2. Of those that a mesh axis runs over, the one named last changes fastest.
Arguments:
- channel: bfloat16 [32768, 32, 3, 128], P('users', 'rb'), may hold values from -13 to 13
- serving: int32 [32768], P('users'), may hold values from 0 to 63, as said below
- interferers: int32 [32768, 2], P('users'), may hold values from 0 to 63, as said below
- plan: int32 [64, 32, 16], P(None, 'rb'), may hold values from 0 to 32767, as said below
- regularizer: float32 [64], P('users'), may hold values from 0.3 to 1.5
- noise_floor: float32 [64], replicated, may hold values from 0.05 to 0.5
Outputs:
- precoders: bfloat16 [64, 32, 16, 128], P('users', 'rb')
- track_metric: float32 [32768, 32], P('users', 'rb')
- entry_rate: float32 [64, 32, 16], P('users', 'rb')
The draws below stay inside these ranges and needn't reach their ends.
Inputs may be any that keep to these rules, and one draw needn't show every extreme that they name: `serving`: each aligned block of 1024 tracks holds exactly 16 tracks served by each cell. `interferers`: A track's 2 interfering cells differ from each other and from its serving cell; each aligned block of 1024 tracks holds exactly 16 tracks with a given cell in a given column. `plan`: each entry names a track served by that cell, and the 16 tracks of a cell on one resource block differ. Take a cell group g (cells g * 2 to g * 2 + 1) and an aligned block of 4 resource blocks: at most 8 of its entries name tracks of one aligned block of 1024 tracks.
All inputs are finite; a program needn't handle non-finite values.
Results may differ from the reference program's by a relative error of at most 0.0035.
Values may be sent and summed in bfloat16 or wider, within the bound.
No kernel may reach another device: no remote copies, remote signals or barrier semaphores. Data moves between devices by JAX's collectives and lax.ppermute only.
A program may use at most 64 MiB of HBM per device.

```python
import math
import jax
import jax.numpy as jnp
from jax import lax

ANTENNA_COUNT = 64
BEAMS = 16
NI = 2
HEARD_CELLS = 3
ITERS = 12
CELL_DEV = 2
CELL_TOTAL = 64
TRACK_DEV = 1024
USER_TRACKS = 32768
SERVED = 16
RB_DEV = 4
RESOURCE_BLOCKS = 32
CAP = 8


def track_layout(key):
    groups = USER_TRACKS // TRACK_DEV
    perm_keys = jax.random.split(jax.random.fold_in(key, 11), groups)
    placement = jax.vmap(lambda one_key: jax.random.permutation(one_key, TRACK_DEV))(perm_keys).astype(jnp.int32)
    home_cell = placement // SERVED
    within = placement % SERVED
    shift_keys = jax.random.split(jax.random.fold_in(key, 12), groups * SERVED)
    shifts = jax.vmap(lambda one_key: jax.random.permutation(one_key, CELL_TOTAL - 1))(shift_keys).astype(jnp.int32)
    shifts = (shifts[:, :NI] + 1).reshape(groups, SERVED, NI)
    group_index = jnp.arange(groups, dtype=jnp.int32)[:, None]
    track_shift = shifts[group_index, within]
    hearing = (home_cell[:, :, None] + track_shift) % CELL_TOTAL
    inverse = jnp.zeros_like(placement).at[group_index, placement].set(jnp.broadcast_to(jnp.arange(TRACK_DEV, dtype=jnp.int32)[None, :], placement.shape))
    return (home_cell.reshape(USER_TRACKS), hearing.reshape(USER_TRACKS, NI), inverse)


def draw_serving(key, part):
    return track_layout(key)[0].astype(jnp.int32)


def draw_interferers(key, part):
    return track_layout(key)[1].astype(jnp.int32)


def draw_plan(key, part):
    groups = USER_TRACKS // TRACK_DEV
    rb_groups = RESOURCE_BLOCKS // RB_DEV
    entries = CELL_DEV * RB_DEV * BEAMS
    half_cap = CAP // 2
    inverse = track_layout(key)[2]
    block_keys = jax.random.split(jax.random.fold_in(key, 21), groups * rb_groups)
    dest_groups = jnp.repeat(jnp.arange(groups, dtype=jnp.int32), rb_groups)
    entry_iota = jnp.arange(entries, dtype=jnp.int32)

    def one_block(block_key, dest_group):
        pair_key, tilt_key, order_key = jax.random.split(block_key, 3)
        pairing = jax.random.permutation(pair_key, groups).astype(jnp.int32)
        tilt_amount = jax.random.randint(tilt_key, (groups // 2,), 0, half_cap + 1).astype(jnp.int32)
        tilt_amount = tilt_amount.at[0].set(half_cap)
        counts = jnp.zeros((groups,), jnp.int32).at[pairing[0::2]].set(half_cap + tilt_amount)
        counts = counts.at[pairing[1::2]].set(half_cap - tilt_amount)
        count_ends = jnp.cumsum(counts)
        sorted_source = jnp.sum((count_ends[None, :] <= entry_iota[:, None]).astype(jnp.int32), axis=1)
        shuffled = sorted_source[jax.random.permutation(order_key, entries)]
        cell_local = entry_iota // (RB_DEV * BEAMS)
        bucket = shuffled * CELL_DEV + cell_local
        bucket_match = (bucket[:, None] == jnp.arange(groups * CELL_DEV, dtype=jnp.int32)[None, :]).astype(jnp.int32)
        slot_rank = jnp.sum((jnp.cumsum(bucket_match, axis=0) - 1) * bucket_match, axis=1)
        cell_global = dest_group * CELL_DEV + cell_local
        return shuffled * TRACK_DEV + inverse[shuffled, cell_global * SERVED + slot_rank]
    table = jax.vmap(one_block)(block_keys, dest_groups)
    table = table.reshape(groups, rb_groups, CELL_DEV, RB_DEV, BEAMS).transpose(0, 2, 1, 3, 4)
    return table.reshape(CELL_TOTAL, RESOURCE_BLOCKS, BEAMS).astype(jnp.int32)


def draw_channel(key, part):
    amp_key, element_key = jax.random.split(key, 2)
    ramp = jnp.arange(RESOURCE_BLOCKS, dtype=jnp.float32) / max(RESOURCE_BLOCKS - 1, 1)
    amplitude = jnp.exp(jax.random.uniform(amp_key, (USER_TRACKS, 1, HEARD_CELLS, 1), jnp.float32, jnp.log(0.3), jnp.log(3.0)))
    profile = 0.6 + 0.8 * ramp
    element_values = jnp.clip(jax.random.normal(element_key, (USER_TRACKS, RESOURCE_BLOCKS, HEARD_CELLS, 2 * ANTENNA_COUNT), jnp.float32), -4.0, 4.0) * 0.70710677
    return (amplitude * profile[None, :, None, None] * element_values).astype(jnp.bfloat16)


def block_levels(rng, extent, pieces, least, largest):
    loudness, own = 1.0, jax.random.fold_in(rng, 6)
    for dim, shards_of in pieces:
        steps = jnp.exp(jax.random.uniform(jax.random.fold_in(own, dim), (shards_of,), jnp.float32, least / len(pieces), largest / len(pieces)))
        loudness = loudness * jnp.repeat(steps, extent[dim] // shards_of).reshape([-1 if axis == dim else 1 for axis in range(len(extent))])
    return loudness


def setup_inputs(seed: int = 0) -> dict:
    key_list = jax.random.split(jax.random.key(seed), 7)
    return {
        "channel": draw_channel(jax.random.fold_in(key_list[6], 71), 0),
        "serving": draw_serving(jax.random.fold_in(key_list[6], 71), 0),
        "interferers": draw_interferers(jax.random.fold_in(key_list[6], 71), 0),
        "plan": draw_plan(jax.random.fold_in(key_list[6], 71), 0),
        "regularizer": jnp.clip(jnp.exp(math.log(1.5) - 1.60943787 * jax.random.uniform(key_list[4], (CELL_TOTAL,), jnp.float32) ** block_levels(key_list[4], (CELL_TOTAL,), ((0, 32),), -0.2, 0.2)), 0.3, 1.5),
        "noise_floor": jnp.clip(jnp.exp(jax.random.uniform(key_list[5], (CELL_TOTAL,), jnp.float32, math.log(0.05), math.log(0.5))), 0.05, 0.5),
    }


HIGH = lax.Precision.HIGHEST

def real_form(beam_rows):
    antennas = beam_rows.shape[-1] // 2
    turned = jnp.concatenate([beam_rows[..., antennas:], -beam_rows[..., :antennas]], axis=-1)
    return jnp.concatenate([beam_rows, turned], axis=-2)

def embed_rows(channel_rows):
    antennas = channel_rows.shape[-1] // 2
    bottom_rows = jnp.concatenate([-channel_rows[..., antennas:], channel_rows[..., :antennas]], axis=-1)
    return jnp.concatenate([channel_rows, bottom_rows], axis=-2)

def unscaled_beams(sched_rows, regularizer):
    beam_count = sched_rows.shape[-2]
    embedded = embed_rows(sched_rows.astype(jnp.float32))
    gram = jnp.einsum('crkd,crjd->crkj', embedded, embedded, precision=HIGH)
    identity = jnp.eye(2 * beam_count, dtype=jnp.float32)
    gram = gram + regularizer[:, None, None, None] * identity
    gram_trace = jnp.trace(gram, axis1=2, axis2=3)
    start_inverse = (2.0 / gram_trace)[:, :, None, None] * identity

    def newton_step(iteration, inverse):
        product = jnp.einsum('crkj,crjl->crkl', gram, inverse, precision=HIGH)
        return 2.0 * inverse - jnp.einsum('crkj,crjl->crkl', inverse, product, precision=HIGH)
    inverse = lax.fori_loop(0, ITERS, newton_step, start_inverse)
    return jnp.einsum('crkd,crkj->crjd', embedded, inverse[..., :beam_count], precision=HIGH)

def reference(channel, serving, interferers, plan, regularizer, noise_floor):
    block_index = jnp.arange(RESOURCE_BLOCKS, dtype=jnp.int32)[None, :, None]
    sched_rows = channel[plan, block_index, 0]
    vectors = unscaled_beams(sched_rows, regularizer)
    cell_power = lax.optimization_barrier(jnp.sum(vectors * vectors, axis=(1, 2, 3)))
    precoders = (vectors * lax.rsqrt(cell_power / RESOURCE_BLOCKS + 1e-06)[:, None, None, None]).astype(jnp.bfloat16)
    forms = real_form(precoders)
    track_iota = jnp.arange(USER_TRACKS, dtype=jnp.int32)
    slot_cells = jnp.concatenate([serving[:, None], interferers], axis=1).T
    orders = jnp.argsort(slot_cells * USER_TRACKS + track_iota[None, :], axis=1).astype(jnp.int32)
    ranks = jnp.zeros_like(orders).at[jnp.arange(HEARD_CELLS, dtype=jnp.int32)[:, None], orders].set(jnp.broadcast_to(track_iota[None, :], orders.shape))
    cell_share = USER_TRACKS // CELL_TOTAL

    def block_powers(block_number):
        form_block = lax.dynamic_index_in_dim(forms, block_number, axis=1, keepdims=False).astype(jnp.float32)
        results = []
        for slot_number in range(HEARD_CELLS):
            track_row_list = channel[orders[slot_number], block_number, slot_number].astype(jnp.float32)
            track_row_list = track_row_list.reshape(CELL_TOTAL, cell_share, 2 * ANTENNA_COUNT)
            projected = jnp.einsum('cpd,ckd->cpk', track_row_list, form_block)
            grouped = lax.optimization_barrier(jnp.sum(projected * projected, axis=-1)).reshape(USER_TRACKS)
            results.append(grouped[ranks[slot_number]])
        return jnp.stack(results)
    powers = lax.map(block_powers, jnp.arange(RESOURCE_BLOCKS, dtype=jnp.int32))
    interference = powers[:, 1]
    for slot_number in range(2, HEARD_CELLS):
        interference = interference + powers[:, slot_number]
    denominator = interference + noise_floor[serving][None, :]
    track_metric = jnp.log2(1.0 + powers[:, 0] / denominator).T
    crossed = jnp.einsum('crkd,crjd->crkj', sched_rows.astype(jnp.float32), forms.astype(jnp.float32))
    magnitude = crossed[..., :BEAMS] * crossed[..., :BEAMS] + crossed[..., BEAMS:] * crossed[..., BEAMS:]
    identity = jnp.eye(BEAMS, dtype=jnp.float32)
    signal = lax.optimization_barrier(jnp.sum(magnitude * identity, axis=-1))
    leakage = lax.optimization_barrier(jnp.sum(magnitude * (1.0 - identity), axis=-1))
    entry_denominator = denominator.T[plan, block_index]
    entry_rate = jnp.log2(1.0 + signal / (leakage + entry_denominator))
    return (precoders, track_metric, entry_rate)
```

```python
import jax
import jax.numpy as jnp
from jax import lax
from jax.experimental import pallas as pl
from jax.experimental.pallas import tpu as pltpu
from jax.sharding import PartitionSpec as P

ITERS = 12
HIGH = lax.Precision.HIGHEST
F32 = jnp.float32
BF16 = jnp.bfloat16
LANES = 128


VM = pl.BlockSpec(memory_space=pltpu.VMEM)
SM = pl.BlockSpec(memory_space=pltpu.SMEM)


def params():
    return pltpu.CompilerParams(vmem_limit_bytes=48 << 20)


def iota(shape, dim):
    return lax.broadcasted_iota(jnp.int32, shape, dim)


def nt(a, b, precision=None):
    return lax.dot_general(
        a, b, (((1,), (1,)), ((), ())), precision=precision, preferred_element_type=F32
    )


def turn(rows):
    rolled = pltpu.roll(rows, 64, 1)
    return jnp.where(iota(rows.shape, 1) < 64, -rolled, rolled)


def lane_pick(values, index):
    return jnp.take_along_axis(values, index, axis=1)


def pack_kernel(send_ref, hear_ref, ch_ref, wide_ref, out_ref, pay_ref):
    rows = ch_ref.shape[0]
    step = 2048
    for start in range(0, rows, step):
        wide_ref[start : start + step, :] = ch_ref[start : start + step, :].astype(F32)
    lane = iota((1, LANES), 1)

    def one(i, carry):
        where = send_ref[i]
        track = where // 12
        for s in range(3):
            pay_ref[s, pl.ds(i, 1), :] = wide_ref[pl.ds(where + 4 * s, 1), :]
        first = hear_ref[0, track]
        second = hear_ref[1, track]
        ids = jnp.where(lane == 0, first, jnp.where(lane == 1, second, 0))
        pay_ref[3, pl.ds(i, 1), :] = ids.astype(F32)
        return carry

    lax.fori_loop(0, send_ref.shape[0], one, 0, unroll=8)
    for s in range(4):
        out_ref[:, s * LANES : (s + 1) * LANES] = pay_ref[s].astype(BF16)


def sort_kernel(serving_ref, hear_ref, wide_ref, hs_ref, ht_ref, pos_ref):
    tracks = serving_ref.shape[1]
    cell_rows = [serving_ref[...], hear_ref[0:1, :], hear_ref[1:2, :]]
    cells = iota((64, LANES), 0)
    upper = (iota((LANES, LANES), 0) < iota((LANES, LANES), 1)).astype(BF16)
    ones = jnp.ones((LANES, LANES), BF16)
    run = jnp.zeros((192, LANES), F32)
    for b in range(tracks // LANES):
        lanes = slice(b * LANES, (b + 1) * LANES)
        hot = jnp.concatenate(
            [(cells == row[:, lanes]).astype(F32) for row in cell_rows], axis=0
        )
        hot16 = hot.astype(BF16)
        count = jnp.dot(hot16, upper, preferred_element_type=F32) + run
        run = run + jnp.dot(hot16, ones, preferred_element_type=F32)
        chosen = hot * count
        for s in range(3):
            rank = jnp.sum(chosen[s * 64 : (s + 1) * 64, :], axis=0, keepdims=True)
            pos_ref[s : s + 1, lanes] = cell_rows[s][:, lanes] * 16 + rank.astype(jnp.int32)
    step = 256
    for s in range(3):
        rows = jnp.concatenate(
            [wide_ref[pl.ds(4 * s + r, tracks, stride=12), :].astype(BF16) for r in range(4)],
            axis=1,
        )
        pos = pos_ref[s : s + 1, :]
        for start in range(0, tracks, step):
            pick = (iota((step, tracks), 0) + start == pos).astype(F32).astype(BF16)
            moved = jnp.dot(pick, rows, preferred_element_type=F32)
            for r in range(4):
                part = moved[:, r * LANES : (r + 1) * LANES]
                hs_ref[s, r, start : start + step, :] = part.astype(BF16)
                ht_ref[s, r, start : start + step, :] = turn(part).astype(BF16)


def beam_kernel(
    pick_ref, arrived_ref, reg_ref, v_ref, h_ref, ht_ref, ei_ref, eit_ref, id_ref, pw_ref,
    gr_ref, gi_ref, xr_ref, xi_ref, tr_ref, ti_ref
):
    pick = (iota((LANES, 256), 1) == pick_ref[...]).astype(F32).astype(BF16)
    rows = jnp.dot(pick, arrived_ref[...], preferred_element_type=F32)
    h = rows[:, :LANES]
    h16 = h.astype(BF16)
    ht = turn(h)
    ht16 = ht.astype(BF16)
    h_ref[...] = h16
    ht_ref[...] = ht16
    s1 = rows[:, LANES : 2 * LANES]
    s2 = rows[:, 2 * LANES : 3 * LANES]
    t1 = turn(s1)
    t2 = turn(s2)
    blank = jnp.zeros((64, LANES), BF16)
    for r in range(4):
        part = slice(r * 32, (r + 1) * 32)
        ei_ref[r] = jnp.concatenate([s1[part].astype(BF16), s2[part].astype(BF16), blank], axis=0)
        eit_ref[r] = jnp.concatenate([t1[part].astype(BF16), t2[part].astype(BF16), blank], axis=0)
    two = (iota((8, LANES), 0) == iota((8, LANES), 1)).astype(F32).astype(BF16)
    id_rows = nt(two, rows[:, 3 * LANES :].astype(BF16))
    none = jnp.full((1, 64), -1.0, F32)
    id_ref[...] = jnp.concatenate(
        [
            jnp.concatenate(
                [id_rows[0:1, r * 32 : (r + 1) * 32], id_rows[1:2, r * 32 : (r + 1) * 32], none], axis=1
            )
            for r in range(4)
        ]
        + [jnp.full((4, LANES), -1.0, F32)],
        axis=0,
    ).astype(jnp.int32)

    full_r = nt(h16, h16)
    full_i = -nt(h16, ht16)
    lane = iota((16, LANES), 1)
    sub = iota((16, LANES), 0)
    gr = jnp.zeros((16, LANES), F32)
    gi = jnp.zeros((16, LANES), F32)
    for m in range(8):
        here = lane // 16 == m
        gr = jnp.where(here, full_r[m * 16 : (m + 1) * 16], gr)
        gi = jnp.where(here, full_i[m * 16 : (m + 1) * 16], gi)
    eye = lane % 16 == sub
    gr = jnp.where(eye, gr + reg_ref[...], gr)
    diag = jnp.sum(jnp.where(eye, gr, 0.0), axis=0, keepdims=True)
    same = (iota((LANES, LANES), 0) // 16 == iota((LANES, LANES), 1) // 16).astype(F32)
    trace = jnp.dot(
        jnp.broadcast_to(diag, (8, LANES)), same, precision=HIGH, preferred_element_type=F32
    )[0:1]
    xr0 = jnp.where(eye, 1.0 / trace, 0.0)
    xi0 = jnp.zeros((16, LANES), F32)
    base = iota((8, LANES), 1) // 16 * 16

    def spread(values, k):
        return jnp.concatenate(
            [lane_pick(values[0:8], base + k), lane_pick(values[8:16], base + k)], axis=0
        )

    for k in range(16):
        gr_ref[k] = spread(gr, k)
        gi_ref[k] = spread(gi, k)

    def product(left, right_r, right_i):
        sums = [None] * 4
        for k in range(16):
            ar, ai = left(k)
            br = jnp.broadcast_to(right_r[k : k + 1], (16, LANES))
            bi = jnp.broadcast_to(right_i[k : k + 1], (16, LANES))
            terms = (ar * br, ai * bi, ar * bi, ai * br)
            sums = [t if a is None else a + t for a, t in zip(sums, terms)]
        return sums[0] - sums[1], sums[2] + sums[3]

    def newton(_, carry):
        xr, xi = carry
        tr, ti = product(lambda k: (gr_ref[k], gi_ref[k]), xr, xi)
        sr, si = product(lambda k: (spread(xr, k), spread(xi, k)), tr, ti)
        return 2.0 * xr - sr, 2.0 * xi - si

    xr, xi = lax.fori_loop(0, ITERS, newton, (xr0, xi0))
    same_block = iota((LANES, LANES), 0) // 16 == iota((LANES, LANES), 1) // 16
    big_r = jnp.where(same_block, jnp.concatenate([xr] * 8, axis=0), 0.0)
    big_i = jnp.where(same_block, jnp.concatenate([xi] * 8, axis=0), 0.0)
    v = jnp.dot(big_r, h, precision=HIGH, preferred_element_type=F32) - jnp.dot(
        big_i, ht, precision=HIGH, preferred_element_type=F32
    )
    v_ref[...] = v
    square = v * v
    for c in range(2):
        part = square[c * 16 : c * 16 + 16]
        for r in range(1, 4):
            part = part + square[r * 32 + c * 16 : r * 32 + c * 16 + 16]
        total = jnp.sum(jnp.sum(part, axis=0, keepdims=True), axis=1, keepdims=True)
        for d in range(8):
            pw_ref[d, c : c + 1, :] = jnp.broadcast_to(total, (1, LANES))


def scale_kernel(v_ref, pw_ref, h_ref, ht_ref, w_ref, send_ref, sl_ref):
    power = pw_ref[0]
    for d in range(1, 8):
        power = power + pw_ref[d]
    scale = lax.rsqrt(power / 32.0 + 1e-06)
    parts = []
    for r in range(4):
        for c in range(2):
            rows = slice(r * 32 + c * 16, r * 32 + c * 16 + 16)
            w = (v_ref[rows, :] * scale[c : c + 1, :]).astype(BF16)
            w_ref[c, r] = w
            parts.append(w)
    w = jnp.concatenate(parts, axis=0)
    for d in range(8):
        for r in range(4):
            send_ref[d, r] = w[r * 32 : (r + 1) * 32]
    re = nt(w, h_ref[...])
    im = nt(w, ht_ref[...])
    mag = re * re + im * im
    row = iota((LANES, LANES), 0)
    col = iota((LANES, LANES), 1)
    signal = jnp.sum(jnp.where(row == col, mag, 0.0), axis=0, keepdims=True)
    other = (row // 16 == col // 16) & (row != col)
    leakage = jnp.sum(jnp.where(other, mag, 0.0), axis=0, keepdims=True)
    sl_ref[...] = jnp.concatenate([signal, leakage, jnp.zeros((6, LANES), F32)], axis=0)


def block_power(w_ref, first_cell, hs_ref, ht_ref, ei_ref, eit_ref, id_ref, y_ref, ent_ref):
    lane = iota((1, 3 * LANES), 1) % LANES // 16
    for r in range(4):
        for half in range(2):
            cell = first_cell + half * 8
            at = pl.ds(pl.multiple_of(cell * 16, LANES), LANES)
            w = w_ref[half * 4 : half * 4 + 4, r].reshape(LANES, LANES)
            plain = jnp.concatenate([hs_ref[s, r, at, :] for s in range(3)] + [ei_ref[r]], axis=0)
            turned = jnp.concatenate([ht_ref[s, r, at, :] for s in range(3)] + [eit_ref[r]], axis=0)
            re = nt(w, plain)
            im = nt(w, turned)
            mag = re * re + im * im
            wanted = jnp.concatenate([lane, id_ref[r : r + 1, :] - cell], axis=1)
            wanted = jnp.broadcast_to(wanted, (8, 4 * LANES))
            total = jnp.zeros((8, 4 * LANES), F32)
            for i in range(8):
                both = mag[i * 16 : i * 16 + 8] + mag[i * 16 + 8 : i * 16 + 16]
                total = total + jnp.where(wanted == i, both, 0.0)
            total = jnp.sum(total, axis=0, keepdims=True)
            for s in range(3):
                y_ref[s, r : r + 1, at] = total[:, s * LANES : (s + 1) * LANES]
            ent_ref[r : r + 1, :] += total[:, 3 * LANES :]


def own_kernel(me_ref, w_ref, hs_ref, ht_ref, ei_ref, eit_ref, id_ref, y_ref, ent_ref):
    y_ref[...] = jnp.zeros_like(y_ref)
    ent_ref[...] = jnp.zeros_like(ent_ref)
    block_power(
        w_ref, me_ref[0] // 8 * 16, hs_ref, ht_ref, ei_ref, eit_ref, id_ref, y_ref, ent_ref
    )


def last_kernel(
    me_ref, w1_ref, w2_ref, w3_ref, hs_ref, ht_ref, ei_ref, eit_ref, id_ref, y0_ref, ent0_ref,
    pos_ref, serving_ref, floor_ref, sl_ref, metric_ref, rate_ref, y_ref, ent_ref
):
    y_ref[...] = y0_ref[...]
    ent_ref[...] = ent0_ref[...]
    mine = me_ref[0] // 8
    for d, w_ref in ((1, w1_ref), (3, w3_ref), (2, w2_ref)):
        source = lax.rem(mine + 4 - d, 4)
        block_power(w_ref, source * 16, hs_ref, ht_ref, ei_ref, eit_ref, id_ref, y_ref, ent_ref)
    floors = jnp.broadcast_to(floor_ref[...], (8, LANES))
    tracks = serving_ref.shape[1]
    for b in range(tracks // LANES):
        lanes = slice(b * LANES, (b + 1) * LANES)
        heard = []
        for s in range(3):
            pos = jnp.broadcast_to(pos_ref[s : s + 1, lanes], (8, LANES))
            low = pos % LANES
            high = pos // LANES
            got = jnp.zeros((8, LANES), F32)
            for q in range(tracks // LANES):
                here = lane_pick(y_ref[s, :, q * LANES : (q + 1) * LANES], low)
                got = jnp.where(high == q, here, got)
            heard.append(got)
        floor = lane_pick(floors, jnp.broadcast_to(serving_ref[:, lanes], (8, LANES)))
        denominator = (heard[1] + heard[2]) + floor
        metric_ref[:, lanes] = jnp.log2(1.0 + heard[0] / denominator)[0:4]
    ent = ent_ref[...]
    sums = ent + pltpu.roll(ent, LANES - 32, 1)
    row = jnp.concatenate([sums[r : r + 1, 0:32] for r in range(4)], axis=1)
    cell = me_ref[0] * 2 + iota((8, LANES), 1) % 32 // 16
    denominator = row + lane_pick(floors, cell)[0:1]
    rate = jnp.log2(1.0 + sl_ref[0:1, :] / (sl_ref[1:2, :] + denominator))
    for r in range(4):
        for c in range(2):
            start = r * 32 + c * 16
            rate_ref[c, r : r + 1, :] = rate[:, start : start + 16]


def shape(dims, dtype=F32):
    return jax.ShapeDtypeStruct(dims, dtype)


def on_device(channel, serving, interferers, plan, regularizer, noise_floor):
    track_dev = channel.shape[0]
    me = lax.axis_index("users")
    me_vec = me.astype(jnp.int32).reshape(1)
    hear = interferers.T
    serving_row = serving.reshape(1, track_dev)
    flat = channel.transpose(0, 2, 1, 3).reshape(track_dev * 12, LANES)

    entries = plan.reshape(32, 2, 4, 16).transpose(0, 2, 1, 3).reshape(32, LANES)
    owned = entries // track_dev == me
    rank = jnp.cumsum(owned.astype(jnp.int32), axis=1) - 1
    rank = jnp.where(owned, rank, 8)
    block = iota((32, LANES), 1) // 32
    where = (entries - me * track_dev) * 12 + block
    match = rank[:, None, :] == jnp.arange(8, dtype=jnp.int32)[None, :, None]
    send = jnp.sum(jnp.where(match, where[:, None, :], 0), axis=2).reshape(256)

    wide, payload = pl.pallas_call(
        pack_kernel,
        out_shape=(shape((track_dev * 12, LANES)), shape((256, 4 * LANES), BF16)),
        in_specs=[SM, SM, VM],
        out_specs=(VM, VM),
        scratch_shapes=[pltpu.VMEM((4, 256, LANES), F32)],
        compiler_params=params(),
        name="pack",
    )(send, hear, flat)
    arrived = lax.all_to_all(
        payload.reshape(32, 8, 4 * LANES), "users", split_axis=0, concat_axis=0, tiled=True
    ).reshape(256, 4 * LANES)

    hs, ht, pos = pl.pallas_call(
        sort_kernel,
        out_shape=(
            shape((3, 4, track_dev, LANES), BF16),
            shape((3, 4, track_dev, LANES), BF16),
            shape((3, track_dev), jnp.int32),
        ),
        in_specs=[VM, VM, VM],
        out_specs=(VM, VM, VM),
        compiler_params=params(),
        name="arrange",
    )(serving_row, hear, wide)

    mine = lax.dynamic_slice_in_dim(entries, me, 1, axis=0)[0]
    source = mine // track_dev
    source_hot = (source[:, None] == jnp.arange(32, dtype=jnp.int32)[None, :]).astype(jnp.int32)
    my_rank = jnp.sum((jnp.cumsum(source_hot, axis=0) - 1) * source_hot, axis=1)
    pick = (source * 8 + my_rank).reshape(LANES, 1)
    reg_row = regularizer[iota((1, LANES), 1) // 16 % 2]

    v, h, h_turn, ei, eit, ids, power = pl.pallas_call(
        beam_kernel,
        out_shape=(
            shape((LANES, LANES)),
            shape((LANES, LANES), BF16),
            shape((LANES, LANES), BF16),
            shape((4, LANES, LANES), BF16),
            shape((4, LANES, LANES), BF16),
            shape((8, LANES), jnp.int32),
            shape((8, 2, LANES)),
        ),
        in_specs=[VM, VM, VM],
        out_specs=(VM,) * 7,
        scratch_shapes=[pltpu.VMEM((16, 16, LANES), F32)] * 2 + [pltpu.VMEM((16, LANES), F32)] * 4,
        compiler_params=params(),
        name="beams",
    )(pick, arrived, reg_row)
    power = lax.all_to_all(power, "rb", split_axis=0, concat_axis=0, tiled=True)

    precoders, outgoing, sl = pl.pallas_call(
        scale_kernel,
        out_shape=(
            shape((2, 4, 16, LANES), BF16),
            shape((8, 4, 32, LANES), BF16),
            shape((8, LANES)),
        ),
        in_specs=[VM] * 4,
        out_specs=(VM,) * 3,
        compiler_params=params(),
        name="scale",
    )(v, power, h, h_turn)

    along_z = [[x * 8 + z for z in range(8)] for x in range(4)]
    own = lax.all_to_all(
        outgoing, "users", split_axis=0, concat_axis=0, axis_index_groups=along_z, tiled=True
    )
    others = [
        lax.ppermute(own, "users", [(u, (u // 8 + d) % 4 * 8 + u % 8) for u in range(32)])
        for d in (1, 2, 3)
    ]
    y0, ent0 = pl.pallas_call(
        own_kernel,
        out_shape=(shape((3, 8, track_dev)), shape((8, LANES))),
        in_specs=[SM] + [VM] * 6,
        out_specs=(VM, VM),
        compiler_params=params(),
        name="own",
    )(me_vec, own, hs, ht, ei, eit, ids)
    floor_row = jnp.pad(noise_floor, (0, 64)).reshape(1, LANES)
    metric, rate = pl.pallas_call(
        last_kernel,
        out_shape=(shape((4, track_dev)), shape((2, 4, 16))),
        in_specs=[SM] + [VM] * 14,
        out_specs=(VM, VM),
        scratch_shapes=[pltpu.VMEM((3, 8, track_dev), F32), pltpu.VMEM((8, LANES), F32)],
        compiler_params=params(),
        name="last",
    )(me_vec, *others, hs, ht, ei, eit, ids, y0, ent0, pos, serving_row, floor_row, sl)
    return (precoders, metric.T, rate)


def solution(mesh):
    return jax.shard_map(
        on_device,
        mesh=mesh,
        in_specs=(
            P("users", "rb", None, None),
            P("users"),
            P("users", None),
            P(None, "rb", None),
            P("users"),
            P(),
        ),
        out_specs=(P("users", "rb", None, None), P("users", "rb"), P("users", "rb", None)),
        check_vma=False,
    )
```

```python
import jax
import jax.numpy as jnp
from jax import lax
from jax.experimental import pallas as pl
from jax.experimental.pallas import tpu as pltpu
from jax.sharding import PartitionSpec as P

ITERS = 12
HIGH = lax.Precision.HIGHEST
F32 = jnp.float32
BF16 = jnp.bfloat16
LANES = 128


VM = pl.BlockSpec(memory_space=pltpu.VMEM)
SM = pl.BlockSpec(memory_space=pltpu.SMEM)


def params():
    return pltpu.CompilerParams(vmem_limit_bytes=24 << 20)


def iota(shape, dim):
    return lax.broadcasted_iota(jnp.int32, shape, dim)


def nt(a, b, precision=None):
    return lax.dot_general(
        a, b, (((1,), (1,)), ((), ())), precision=precision, preferred_element_type=F32
    )


def turn(rows):
    rolled = pltpu.roll(rows, 64, 1)
    return jnp.where(iota(rows.shape, 1) < 64, -rolled, rolled)


def lane_pick(values, index):
    return jnp.take_along_axis(values, index, axis=1)


def gather_kernel(
    me_ref, plan_ref, hear_ref, ch_ref, out_ref, pick_ref, buf_ref, wide_ref, code_ref, list_ref,
    list_sem, row_sem
):
    me = me_ref[0]
    plan = plan_ref[...]
    cells = plan.shape[1]
    tracks = hear_ref.shape[1]
    local = plan - me * tracks
    owned = (local >= 0) & (local < tracks)
    hot = owned.astype(F32).astype(BF16)
    row = iota((64, 64), 0)
    col = iota((64, 64), 1)
    before = (col < row).astype(F32).astype(BF16)
    pair = (row // 2 == col // 2).astype(F32).astype(BF16)
    left = ((row + 1 == col) & (col % 2 == 1)).astype(F32).astype(BF16)
    earlier = jnp.dot(before, hot, preferred_element_type=F32).astype(BF16)
    rank = jnp.dot(earlier, pair, preferred_element_type=F32) + jnp.dot(
        hot, left, preferred_element_type=F32
    )
    code = (local * 4 + row // 16).astype(F32)
    codes = jnp.concatenate(
        [
            jnp.sum(jnp.where(owned & (rank == k), code, 0.0), axis=0, keepdims=True)
            for k in range(8)
        ],
        axis=0,
    )
    fold = (iota((cells, LANES), 0) // 2 == iota((cells, LANES), 1)).astype(F32)
    codes = jnp.dot(codes, fold, precision=HIGH, preferred_element_type=F32)
    code_ref[...] = codes.astype(jnp.int32)
    copy = pltpu.make_async_copy(code_ref, list_ref, list_sem)
    copy.start()
    copy.wait()

    def group(g, carry):
        for k in range(8):
            track = lax.shift_right_logical(list_ref[k, g], 2)
            first = pl.multiple_of(track * 12 - 4 * (track & 1), 8)
            slot = pl.multiple_of((g * 8 + k) * 16, 16)
            pltpu.make_async_copy(
                ch_ref.at[pl.ds(first, 16)], buf_ref.at[pl.ds(slot, 16)], row_sem
            ).start()
        return carry

    lax.fori_loop(0, 32, group, 0)

    slot_row = iota((256, LANES), 0)
    slot_lane = iota((256, LANES), 1)
    spread = nt((slot_lane == slot_row // 8).astype(F32), codes, HIGH)
    mine = iota((256, 8), 1) == iota((256, 8), 0) % 8
    column = jnp.sum(jnp.where(mine, spread, 0.0), axis=1, keepdims=True).astype(jnp.int32)
    track = lax.shift_right_logical(column, 2)
    offset = 4 * (track & 1) + (column & 3)
    heard = jnp.concatenate([hear_ref[...].astype(F32), jnp.zeros((6, tracks), F32)], axis=0)
    choose = (iota((256, tracks), 1) == track).astype(F32).astype(BF16)
    ids = nt(choose, heard.astype(BF16))
    out_ref[:, 3 * LANES :] = jnp.concatenate([ids, jnp.zeros((256, 120), F32)], axis=1).astype(BF16)

    sources = []
    for c in range(2):
        values = jnp.sum(jnp.where(col == me * 2 + c, plan, 0), axis=1, keepdims=True)
        sources.append(lax.shift_right_logical(values, 10))
    lane = iota((64, LANES), 1)
    hots = [(lane == source).astype(F32) for source in sources]
    earlier = jnp.dot(before, (hots[0] + hots[1]).astype(BF16), preferred_element_type=F32)
    ranks = [hots[0] * earlier, hots[1] * (earlier + hots[0])]
    picks = [
        source * 8 + jnp.sum(rank, axis=1, keepdims=True).astype(jnp.int32)
        for source, rank in zip(sources, ranks)
    ]
    pick_ref[...] = jnp.concatenate(
        [picks[c][r * 16 : (r + 1) * 16] for r in range(4) for c in range(2)], axis=0
    )

    pltpu.make_async_copy(ch_ref.at[pl.ds(0, 4096)], buf_ref, row_sem).wait()
    wide_ref[...] = buf_ref[...].astype(F32)
    found = [jnp.zeros((256, LANES), F32)] * 3
    for at in range(16):
        rows = wide_ref[pl.ds(at, 256, stride=16), :]
        for s in range(3):
            if 0 <= at - 4 * s < 8:
                found[s] = jnp.where(offset == at - 4 * s, rows, found[s])
    for s in range(3):
        out_ref[:, s * LANES : (s + 1) * LANES] = found[s].astype(BF16)


def sort_kernel(serving_ref, hear_ref, ch_ref, hs_ref, pos_ref, wide_ref):
    tracks = serving_ref.shape[1]
    for start in range(0, ch_ref.shape[0], 2048):
        wide_ref[start : start + 2048, :] = ch_ref[start : start + 2048, :].astype(F32)
    cell_rows = [serving_ref[...], hear_ref[0:1, :], hear_ref[1:2, :]]
    cells = iota((64, LANES), 0)
    upper = (iota((LANES, LANES), 0) < iota((LANES, LANES), 1)).astype(BF16)
    ones = jnp.ones((LANES, LANES), BF16)
    run = jnp.zeros((192, LANES), F32)
    for b in range(tracks // LANES):
        lanes = slice(b * LANES, (b + 1) * LANES)
        hot = jnp.concatenate(
            [(cells == row[:, lanes]).astype(F32) for row in cell_rows], axis=0
        )
        hot16 = hot.astype(BF16)
        count = jnp.dot(hot16, upper, preferred_element_type=F32) + run
        run = run + jnp.dot(hot16, ones, preferred_element_type=F32)
        chosen = hot * count
        for s in range(3):
            rank = jnp.sum(chosen[s * 64 : (s + 1) * 64, :], axis=0, keepdims=True)
            pos_ref[s : s + 1, lanes] = cell_rows[s][:, lanes] * 16 + rank.astype(jnp.int32)
    step = 256
    for s in range(3):
        rows = jnp.concatenate(
            [wide_ref[pl.ds(4 * s + r, tracks, stride=12), :].astype(BF16) for r in range(4)],
            axis=1,
        )
        pos = pos_ref[s : s + 1, :]
        for start in range(0, tracks, step):
            pick = (iota((step, tracks), 0) + start == pos).astype(F32).astype(BF16)
            moved = jnp.dot(pick, rows, preferred_element_type=F32)
            for r in range(4):
                part = moved[:, r * LANES : (r + 1) * LANES]
                hs_ref[s, r, start : start + step, :] = part.astype(BF16)


def beam_kernel(
    reg_ref, pick_ref, arrived_ref, pos_ref, v_ref, h_ref, ht_ref, ei_ref, id_ref,
    pw_ref, gr_ref, gi_ref
):
    pick = (iota((LANES, 256), 1) == pick_ref[...]).astype(F32).astype(BF16)
    rows = jnp.dot(pick, arrived_ref[...], preferred_element_type=F32)
    h = rows[:, :LANES]
    h16 = h.astype(BF16)
    ht = turn(h)
    ht16 = ht.astype(BF16)
    h_ref[...] = h16
    ht_ref[...] = ht16
    s1 = rows[:, LANES : 2 * LANES]
    s2 = rows[:, 2 * LANES : 3 * LANES]
    blank = jnp.zeros((64, LANES), BF16)
    for r in range(4):
        part = slice(r * 32, (r + 1) * 32)
        ei_ref[r] = jnp.concatenate([s1[part].astype(BF16), s2[part].astype(BF16), blank], axis=0)
    two = (iota((8, LANES), 0) == iota((8, LANES), 1)).astype(F32).astype(BF16)
    id_rows = nt(two, rows[:, 3 * LANES :].astype(BF16))
    none = jnp.full((1, 64), -1.0, F32)
    id_ref[...] = jnp.concatenate(
        [
            jnp.concatenate(
                [id_rows[0:1, r * 32 : (r + 1) * 32], id_rows[1:2, r * 32 : (r + 1) * 32], none], axis=1
            )
            for r in range(4)
        ]
        + [jnp.full((4, LANES), -1.0, F32)],
        axis=0,
    ).astype(jnp.int32)

    full_r = nt(h16, h16)
    full_i = -nt(h16, ht16)
    lane = iota((16, LANES), 1)
    sub = iota((16, LANES), 0)
    gr = jnp.zeros((16, LANES), F32)
    gi = jnp.zeros((16, LANES), F32)
    for m in range(8):
        here = lane // 16 == m
        gr = jnp.where(here, full_r[m * 16 : (m + 1) * 16], gr)
        gi = jnp.where(here, full_i[m * 16 : (m + 1) * 16], gi)
    eye = lane % 16 == sub
    reg = jnp.where(lane // 16 % 2 == 0, reg_ref[0], reg_ref[1])
    gr = jnp.where(eye, gr + reg, gr)
    diag = jnp.sum(jnp.where(eye, gr, 0.0), axis=0, keepdims=True)
    same = (iota((LANES, LANES), 0) // 16 == iota((LANES, LANES), 1) // 16).astype(F32)
    trace = jnp.dot(
        jnp.broadcast_to(diag, (8, LANES)), same, precision=HIGH, preferred_element_type=F32
    )[0:1]
    xr0 = jnp.where(eye, 1.0 / trace, 0.0)
    xi0 = jnp.zeros((16, LANES), F32)
    base = iota((8, LANES), 1) // 16 * 16

    def spread(values, k):
        return jnp.concatenate(
            [lane_pick(values[0:8], base + k), lane_pick(values[8:16], base + k)], axis=0
        )

    for k in range(16):
        gr_ref[k] = spread(gr, k)
        gi_ref[k] = spread(gi, k)

    def product(left, right_r, right_i):
        sums = [None] * 4
        for k in range(16):
            ar, ai = left(k)
            br = jnp.broadcast_to(right_r[k : k + 1], (16, LANES))
            bi = jnp.broadcast_to(right_i[k : k + 1], (16, LANES))
            terms = (ar * br, ai * bi, ar * bi, ai * br)
            sums = [t if a is None else a + t for a, t in zip(sums, terms)]
        return sums[0] - sums[1], sums[2] + sums[3]

    def newton(_, carry):
        xr, xi = carry
        tr, ti = product(lambda k: (gr_ref[k], gi_ref[k]), xr, xi)
        sr, si = product(lambda k: (spread(xr, k), spread(xi, k)), tr, ti)
        return 2.0 * xr - sr, 2.0 * xi - si

    xr, xi = lax.fori_loop(0, ITERS, newton, (xr0, xi0))
    same_block = iota((LANES, LANES), 0) // 16 == iota((LANES, LANES), 1) // 16
    big_r = jnp.where(same_block, jnp.concatenate([xr] * 8, axis=0), 0.0)
    big_i = jnp.where(same_block, jnp.concatenate([xi] * 8, axis=0), 0.0)
    v = jnp.dot(big_r, h, precision=HIGH, preferred_element_type=F32) - jnp.dot(
        big_i, ht, precision=HIGH, preferred_element_type=F32
    )
    v_ref[...] = v
    square = v * v
    totals = []
    for c in range(2):
        part = square[c * 16 : c * 16 + 16]
        for r in range(1, 4):
            part = part + square[r * 32 + c * 16 : r * 32 + c * 16 + 16]
        totals.append(jnp.sum(jnp.sum(part, axis=0, keepdims=True), axis=1, keepdims=True))
    for d in range(8):
        for c in range(2):
            pw_ref[d, c : c + 1, :] = jnp.broadcast_to(totals[c], (1, LANES))


def scale_kernel(v_ref, pw_ref, h_ref, ht_ref, w_ref, send_ref, sl_ref):
    power = pw_ref[0]
    for d in range(1, 8):
        power = power + pw_ref[d]
    scale = lax.rsqrt(power / 32.0 + 1e-06)
    parts = []
    for r in range(4):
        for c in range(2):
            rows = slice(r * 32 + c * 16, r * 32 + c * 16 + 16)
            w = (v_ref[rows, :] * scale[c : c + 1, :]).astype(BF16)
            w_ref[c, r] = w
            parts.append(w)
    w = jnp.concatenate(parts, axis=0)
    for d in range(8):
        for r in range(4):
            send_ref[d, r] = w[r * 32 : (r + 1) * 32]
    re = nt(w, h_ref[...])
    im = nt(w, ht_ref[...])
    mag = re * re + im * im
    row = iota((LANES, LANES), 0)
    col = iota((LANES, LANES), 1)
    signal = jnp.sum(jnp.where(row == col, mag, 0.0), axis=0, keepdims=True)
    other = (row // 16 == col // 16) & (row != col)
    leakage = jnp.sum(jnp.where(other, mag, 0.0), axis=0, keepdims=True)
    sl_ref[...] = jnp.concatenate([signal, leakage, jnp.zeros((6, LANES), F32)], axis=0)


def block_power(w_ref, first_cell, hs_ref, ei_ref, id_ref, y_ref, ent_ref):
    lane = iota((1, 3 * LANES), 1) % LANES // 16
    for r in range(4):
        for half in range(2):
            cell = first_cell + half * 8
            at = pl.ds(pl.multiple_of(cell * 16, LANES), LANES)
            w = w_ref[half * 4 : half * 4 + 4, r].reshape(LANES, LANES)
            w_turn = turn(w.astype(F32)).astype(BF16)
            plain = jnp.concatenate([hs_ref[s, r, at, :] for s in range(3)] + [ei_ref[r]], axis=0)
            re = nt(w, plain)
            im = nt(w_turn, plain)
            mag = re * re + im * im
            wanted = jnp.concatenate([lane, id_ref[r : r + 1, :] - cell], axis=1)
            wanted = jnp.broadcast_to(wanted, (8, 4 * LANES))
            total = jnp.zeros((8, 4 * LANES), F32)
            for i in range(8):
                both = mag[i * 16 : i * 16 + 8] + mag[i * 16 + 8 : i * 16 + 16]
                total = total + jnp.where(wanted == i, both, 0.0)
            total = jnp.sum(total, axis=0, keepdims=True)
            for s in range(3):
                y_ref[s, r : r + 1, at] = total[:, s * LANES : (s + 1) * LANES]
            ent_ref[r : r + 1, :] += total[:, 3 * LANES :]


def own_kernel(me_ref, w_ref, hs_ref, ei_ref, id_ref, y_ref, ent_ref):
    y_ref[...] = jnp.zeros_like(y_ref)
    ent_ref[...] = jnp.zeros_like(ent_ref)
    block_power(
        w_ref, me_ref[0] // 8 * 16, hs_ref, ei_ref, id_ref, y_ref, ent_ref
    )


def last_kernel(
    me_ref, w1_ref, w2_ref, w3_ref, hs_ref, ei_ref, id_ref, y0_ref, ent0_ref,
    pos_ref, serving_ref, floor_ref, sl_ref, metric_ref, rate_ref, y_ref, ent_ref
):
    y_ref[...] = y0_ref[...]
    ent_ref[...] = ent0_ref[...]
    mine = me_ref[0] // 8
    for d, w_ref in ((1, w1_ref), (3, w3_ref), (2, w2_ref)):
        source = lax.rem(mine + 4 - d, 4)
        block_power(w_ref, source * 16, hs_ref, ei_ref, id_ref, y_ref, ent_ref)
    floors = jnp.concatenate([floor_ref[...], jnp.zeros((1, 64), F32)], axis=1)
    floors = jnp.broadcast_to(floors, (8, LANES))
    tracks = serving_ref.shape[1]
    for b in range(tracks // LANES):
        lanes = slice(b * LANES, (b + 1) * LANES)
        heard = []
        for s in range(3):
            pos = jnp.broadcast_to(pos_ref[s : s + 1, lanes], (8, LANES))
            low = pos % LANES
            high = pos // LANES
            got = jnp.zeros((8, LANES), F32)
            for q in range(tracks // LANES):
                here = lane_pick(y_ref[s, :, q * LANES : (q + 1) * LANES], low)
                got = jnp.where(high == q, here, got)
            heard.append(got)
        floor = lane_pick(floors, jnp.broadcast_to(serving_ref[:, lanes], (8, LANES)))
        denominator = (heard[1] + heard[2]) + floor
        metric_ref[:, lanes] = jnp.log2(1.0 + heard[0] / denominator)[0:4]
    ent = ent_ref[...]
    sums = ent + pltpu.roll(ent, LANES - 32, 1)
    row = jnp.concatenate([sums[r : r + 1, 0:32] for r in range(4)], axis=1)
    cell = me_ref[0] * 2 + iota((8, LANES), 1) % 32 // 16
    denominator = row + lane_pick(floors, cell)[0:1]
    rate = jnp.log2(1.0 + sl_ref[0:1, :] / (sl_ref[1:2, :] + denominator))
    for r in range(4):
        for c in range(2):
            start = r * 32 + c * 16
            rate_ref[c, r : r + 1, :] = rate[:, start : start + 16]


def shape(dims, dtype=F32):
    return jax.ShapeDtypeStruct(dims, dtype)


def on_device(channel, serving, interferers, plan, regularizer, noise_floor):
    track_dev = channel.shape[0]
    me = lax.axis_index("users")
    me_vec = me.astype(jnp.int32).reshape(1)
    hear = interferers.T
    serving_row = serving.reshape(1, track_dev)
    flat = channel.transpose(0, 2, 1, 3).reshape(track_dev * 12, LANES)

    arrivals = plan.transpose(1, 2, 0).reshape(64, 64)
    payload, pick = pl.pallas_call(
        gather_kernel,
        out_shape=(shape((256, 4 * LANES), BF16), shape((LANES, 1), jnp.int32)),
        in_specs=[SM, VM, VM, pl.BlockSpec(memory_space=pltpu.HBM)],
        out_specs=(VM, VM),
        scratch_shapes=[
            pltpu.VMEM((4096, LANES), BF16),
            pltpu.VMEM((4096, LANES), F32),
            pltpu.VMEM((8, LANES), jnp.int32),
            pltpu.SMEM((8, LANES), jnp.int32),
            pltpu.SemaphoreType.DMA,
            pltpu.SemaphoreType.DMA,
        ],
        compiler_params=params(),
        name="collect",
    )(me_vec, arrivals, hear, pltpu.with_memory_space_constraint(flat, pltpu.HBM))
    arrived = lax.all_to_all(
        payload.reshape(32, 8, 4 * LANES), "users", split_axis=0, concat_axis=0, tiled=True
    ).reshape(256, 4 * LANES)

    hs, pos = pl.pallas_call(
        sort_kernel,
        out_shape=(
            shape((3, 4, track_dev, LANES), BF16),
            shape((3, track_dev), jnp.int32),
        ),
        in_specs=[VM, VM, VM],
        out_specs=(VM, VM),
        scratch_shapes=[pltpu.VMEM((track_dev * 12, LANES), F32)],
        compiler_params=params(),
        name="arrange",
    )(serving_row, hear, flat)

    v, h, h_turn, ei, ids, power = pl.pallas_call(
        beam_kernel,
        out_shape=(
            shape((LANES, LANES)),
            shape((LANES, LANES), BF16),
            shape((LANES, LANES), BF16),
            shape((4, LANES, LANES), BF16),
            shape((8, LANES), jnp.int32),
            shape((8, 2, LANES)),
        ),
        in_specs=[SM, VM, VM, VM],
        out_specs=(VM,) * 6,
        scratch_shapes=[pltpu.VMEM((16, 16, LANES), F32)] * 2,
        compiler_params=params(),
        name="beams",
    )(regularizer, pick, arrived, pos)
    power = lax.all_to_all(power, "rb", split_axis=0, concat_axis=0, tiled=True)

    precoders, outgoing, sl = pl.pallas_call(
        scale_kernel,
        out_shape=(
            shape((2, 4, 16, LANES), BF16),
            shape((8, 4, 32, LANES), BF16),
            shape((8, LANES)),
        ),
        in_specs=[VM] * 4,
        out_specs=(VM,) * 3,
        compiler_params=params(),
        name="scale",
    )(v, power, h, h_turn)

    along_z = [[x * 8 + z for z in range(8)] for x in range(4)]
    own = lax.all_to_all(
        outgoing, "users", split_axis=0, concat_axis=0, axis_index_groups=along_z, tiled=True
    )
    others = [
        lax.ppermute(own, "users", [(u, (u // 8 + d) % 4 * 8 + u % 8) for u in range(32)])
        for d in (1, 2, 3)
    ]
    y0, ent0 = pl.pallas_call(
        own_kernel,
        out_shape=(shape((3, 8, track_dev)), shape((8, LANES))),
        in_specs=[SM] + [VM] * 4,
        out_specs=(VM, VM),
        compiler_params=params(),
        name="own",
    )(me_vec, own, hs, ei, ids)
    floor_row = noise_floor.reshape(1, 64)
    metric, rate = pl.pallas_call(
        last_kernel,
        out_shape=(shape((4, track_dev)), shape((2, 4, 16))),
        in_specs=[SM] + [VM] * 12,
        out_specs=(VM, VM),
        scratch_shapes=[pltpu.VMEM((3, 8, track_dev), F32), pltpu.VMEM((8, LANES), F32)],
        compiler_params=params(),
        name="last",
    )(me_vec, *others, hs, ei, ids, y0, ent0, pos, serving_row, floor_row, sl)
    return (precoders, metric.T, rate)


def solution(mesh):
    step = jax.shard_map(
        on_device,
        mesh=mesh,
        in_specs=(
            P("users", "rb", None, None),
            P("users"),
            P("users", None),
            P(None, "rb", None),
            P("users"),
            P(),
        ),
        out_specs=(P("users", "rb", None, None), P("users", "rb"), P("users", "rb", None)),
        check_vma=False,
    )
    return step
```
